32 devices in a mesh: ctx: 8 (over z, x), fsdp: 4 (over y, core).
Axes of the slice: x: 2, y: 2, z: 4, core: 2. Of those that a mesh axis runs over, the one named last changes fastest.
Arguments:
- acts: bfloat16 [16384, 4096], P(('ctx', 'fsdp')), may hold values from -64 to 64
- queries: bfloat16 [16384, 2048], P(('ctx', 'fsdp')), may hold values from -120 to 120
- kv_weight: bfloat16 [4096, 4, 2, 128], P(None, 'fsdp'), may hold values from -1 to 1
- rand_blocks: int32 [128, 3], replicated, may hold values from 0 to 127, as said below
Outputs:
- attended: bfloat16 [16384, 2048], P(('ctx', 'fsdp'))
The draws below stay inside these ranges and needn't reach their ends.
Inputs may be any that keep to these rules, and one draw needn't show every extreme that they name: `rand_blocks`: call the 16 consecutive blocks of one index of ctx a context shard. Among the 48 entries of the rows of one context shard, the blocks of any one context shard are named at most 6 times in all, and some context shard is named exactly 6 times.
All inputs are finite; a program needn't handle non-finite values.
Results may differ from the reference program's by a relative error of at most 0.0086.
Values may be sent and summed in bfloat16 or wider, within the bound.
No kernel may reach another device: no remote copies, remote signals or barrier semaphores. Data moves between devices by JAX's collectives and lax.ppermute only.
A program may use at most 128 MiB of HBM per device.

```python
import math
import jax
import jax.numpy as jnp
from jax import lax

MODEL_DIM = 4096
QUERY_HEADS = 16
KEY_VALUE_HEADS = 4
HEAD_DIM = 128
BLOCK = 128
GLOBAL = 2
RAND = 3
TOK_DEV = 512
NB = 128
CAP = 6
N_CTX = 8
N_FSDP = 4


def common_weight(key):
    random_draws = jax.random.normal(jax.random.fold_in(key, 7), (MODEL_DIM, KEY_VALUE_HEADS, 2, HEAD_DIM), jnp.float32)
    return jnp.clip(random_draws, -6.0, 6.0) / math.sqrt(MODEL_DIM)


def draw_acts(key, part):
    random_draws = jnp.clip(jax.random.normal(jax.random.fold_in(key, 3), (NB, BLOCK, MODEL_DIM), jnp.float32), -6.0, 6.0)
    return random_draws.reshape(NB * BLOCK, MODEL_DIM).astype(jnp.bfloat16)


def draw_queries(key, part):
    random_draws = jnp.clip(jax.random.normal(jax.random.fold_in(key, 5), (NB, BLOCK, QUERY_HEADS, HEAD_DIM), jnp.float32), -6.0, 6.0)
    return random_draws.reshape(NB * BLOCK, QUERY_HEADS * HEAD_DIM).astype(jnp.bfloat16)


def draw_kv_weight(key, part):
    return common_weight(key).astype(jnp.bfloat16)


def draw_rand_blocks(key, part):
    shard_count = TOK_DEV * N_FSDP // BLOCK
    entries = shard_count * RAND
    shard_keys = jax.random.split(jax.random.fold_in(key, 9), N_CTX)
    source_pool = jnp.arange(N_CTX * CAP, dtype=jnp.int32) % N_CTX

    def draw_shard(shard_key):
        shuffled = jax.random.permutation(shard_key, N_CTX * CAP)
        return source_pool[shuffled[:entries]]
    sources = jax.vmap(draw_shard)(shard_keys)
    offsets = jax.random.randint(jax.random.fold_in(key, 10), (N_CTX, entries), 0, shard_count, dtype=jnp.int32)
    return (sources * shard_count + offsets).reshape(NB, RAND).astype(jnp.int32)


def setup_inputs(seed: int = 0) -> dict:
    key_list = jax.random.split(jax.random.key(seed), 5)
    return {
        "acts": draw_acts(jax.random.fold_in(key_list[4], 71), 0),
        "queries": draw_queries(jax.random.fold_in(key_list[4], 71), 0),
        "kv_weight": draw_kv_weight(jax.random.fold_in(key_list[4], 71), 0),
        "rand_blocks": draw_rand_blocks(jax.random.fold_in(key_list[4], 71), 0),
    }


def reference(acts, queries, kv_weight, rand_blocks):
    token_count = acts.shape[0]
    block_count = token_count // BLOCK
    kv_heads = kv_weight.shape[1]
    head_size = kv_weight.shape[3]
    group_size = queries.shape[1] // head_size // kv_heads
    flat_weight = kv_weight.reshape(MODEL_DIM, kv_heads * 2 * head_size)

    def project(block_rows):
        return jnp.dot(block_rows, flat_weight, preferred_element_type=jnp.float32).astype(jnp.bfloat16)
    key_value = lax.map(project, acts.reshape(block_count, BLOCK, MODEL_DIM))
    key_value = key_value.reshape(block_count, BLOCK, kv_heads, 2, head_size)
    block_ids = jnp.arange(block_count, dtype=jnp.int32)
    fixed_lists = [(block_ids + block_count - 1) % block_count, block_ids, (block_ids + 1) % block_count]
    for global_id in range(GLOBAL):
        fixed_lists.append(jnp.full((block_count,), global_id, dtype=jnp.int32))
    key_ids = jnp.concatenate([jnp.stack(fixed_lists, axis=1), rand_blocks.astype(jnp.int32)], axis=1)
    query_blocks = queries.reshape(block_count, BLOCK, kv_heads, group_size, head_size)
    scale = 1.0 / math.sqrt(head_size)

    def attend(operands):
        query_part, row_ids = operands
        chosen = key_value[row_ids]
        key_rows = chosen[:, :, :, 0, :].reshape(-1, kv_heads, head_size).astype(jnp.float32)
        values = chosen[:, :, :, 1, :].reshape(-1, kv_heads, head_size).astype(jnp.float32)
        scores = jnp.einsum('qhgd,khd->hgqk', query_part.astype(jnp.float32), key_rows) * scale
        largest = lax.optimization_barrier(jnp.max(scores, axis=-1, keepdims=True))
        weights = jnp.exp(scores - largest)
        probs = (weights / lax.optimization_barrier(jnp.sum(weights, axis=-1, keepdims=True))).astype(jnp.bfloat16)
        result = jnp.einsum('hgqk,khd->qhgd', probs.astype(jnp.float32), values)
        return result.astype(jnp.bfloat16).reshape(BLOCK, kv_heads * group_size * head_size)
    attended = lax.map(attend, (query_blocks, key_ids))
    return attended.reshape(token_count, kv_heads * group_size * head_size)
```

```python
import functools
import math

import jax
import jax.numpy as jnp
from jax import lax
from jax.experimental import pallas as pl
from jax.experimental.pallas import tpu as pltpu
from jax.sharding import PartitionSpec as P

BLOCK = 128
GLOBAL = 2
RAND = 3
MOST_PERMUTES = 16


ANY = pl.BlockSpec(memory_space=pl.ANY)


def swap(value, axis, bit):
    size = lax.axis_size(axis)
    return lax.ppermute(value, axis, [(i, i ^ bit) for i in range(size)])


def after(value, *earlier):
    return lax.optimization_barrier((value, *earlier))[0]


def move_blocks(table, sources, out_sizes, by_target, name):
    shape = sources[0].shape[1:]
    dtype = sources[0].dtype
    source_sizes = [s.shape[0] for s in sources]
    fixed_sizes, moving_sizes = (source_sizes, out_sizes) if by_target else (out_sizes, source_sizes)
    slots = sum(fixed_sizes)

    def body(tab, *refs):
        ins, outs, sems = refs[: len(sources)], refs[len(sources) : -1], refs[-1]
        fixed, moving = (ins, outs) if by_target else (outs, ins)
        pairs = [(ref, j) for ref, size in zip(fixed, fixed_sizes) for j in range(size)]
        for t, (ref, j) in enumerate(pairs):
            where = tab[t]
            low = 0
            for other, size in zip(moving, moving_sizes):
                @pl.when((where >= low) & (where < low + size))
                def _(other=other, low=low, ref=ref, j=j, t=t, where=where):
                    ends = (ref.at[j], other.at[where - low])
                    if not by_target:
                        ends = ends[::-1]
                    pltpu.make_async_copy(*ends, sems.at[t]).start()
                low += size
        for t, (ref, j) in enumerate(pairs):
            where = tab[t]
            @pl.when(where >= 0)
            def _(t=t):
                pltpu.make_async_copy(ins[0].at[0], outs[0].at[0], sems.at[t]).wait()

    return pl.pallas_call(
        body,
        grid_spec=pltpu.PrefetchScalarGridSpec(
            num_scalar_prefetch=1,
            grid=(1,),
            in_specs=[ANY] * len(sources),
            out_specs=[ANY] * len(out_sizes),
            scratch_shapes=[pltpu.SemaphoreType.DMA((slots,))],
        ),
        out_shape=[jax.ShapeDtypeStruct((size, *shape), dtype) for size in out_sizes],
        name=name,
    )(table, *sources)


def project(acts_pair, weight, name):
    rows, width = acts_pair[0].shape
    cols = weight.shape[1]
    parts = 2
    step = width // parts

    def body(mine, theirs, w, out, acc):
        turn, part = pl.program_id(0), pl.program_id(1)

        def add(ref):
            term = jnp.dot(ref[...], w[pl.ds(part * step, step), :], preferred_element_type=jnp.float32)

            @pl.when(part == 0)
            def _():
                acc[...] = term

            @pl.when(part == parts - 1)
            def _():
                out[...] = (acc[...] + term).astype(out.dtype)

        pl.when(turn == 0)(lambda: add(mine))
        pl.when(turn == 1)(lambda: add(theirs))

    return pl.pallas_call(
        body,
        grid=(2, parts),
        in_specs=[
            pl.BlockSpec((rows, step), lambda i, k: (0, jnp.where(i == 0, k, parts - 1))),
            pl.BlockSpec((rows, step), lambda i, k: (0, jnp.where(i == 0, 0, k))),
            pl.BlockSpec((width, cols), lambda i, k: (0, 0)),
        ],
        out_specs=pl.BlockSpec((rows, cols), lambda i, k: (i, 0)),
        out_shape=jax.ShapeDtypeStruct((2 * rows, cols), jnp.bfloat16),
        scratch_shapes=[pltpu.VMEM((rows, cols), jnp.float32)],
        name=name,
    )(*acts_pair, weight)


def whole(array):
    zeros = (0,) * array.ndim
    return pl.BlockSpec(array.shape, lambda i, t: zeros)


def probabilities(place, query, key_main, val_main, halo_before, halo_after, globs, key_rand, side, turn, name):
    head_size = key_main.shape[-1]
    chip_blocks = key_main.shape[0]
    per_device = chip_blocks // 2
    rows = query.shape[0]
    group = query.shape[1] // head_size // place["heads"]
    fixed_len = (3 + GLOBAL) * BLOCK
    rand_len = RAND * BLOCK
    factor = 1.0 / math.sqrt(head_size)
    halo_at = 1 - turn

    def body(tab, q_ref, k_ref, v_ref, hb_ref, ha_ref, g_ref, kr_ref, acc_ref, p_ref, kbuf, vbuf):
        i = pl.program_id(0)
        core = tab[0]
        spot = (side ^ core) * per_device + i

        def put(slot, key, value):
            kbuf[pl.ds(slot * BLOCK, BLOCK), :] = key
            vbuf[pl.ds(slot * BLOCK, BLOCK), :] = value

        for slot in range(3):
            at = spot + slot - 1

            @pl.when(at < 0)
            def _(slot=slot):
                put(slot, hb_ref[2 * halo_at], hb_ref[2 * halo_at + 1])

            @pl.when(at >= chip_blocks)
            def _(slot=slot):
                put(slot, ha_ref[2 * halo_at], ha_ref[2 * halo_at + 1])

            @pl.when((at >= 0) & (at < chip_blocks))
            def _(slot=slot, at=at):
                where = ((at // per_device) ^ core) * per_device + at % per_device
                put(slot, k_ref[where], v_ref[where])
        for g in range(GLOBAL):
            put(3 + g, g_ref[g], g_ref[GLOBAL + g])
        for r in range(RAND):
            kbuf[fixed_len + r * BLOCK : fixed_len + (r + 1) * BLOCK, :] = kr_ref[r]
        for h in range(group):
            q = q_ref[:, h * head_size : (h + 1) * head_size]
            scores = lax.dot_general(q, kbuf[...], (((1,), (1,)), ((), ())), preferred_element_type=jnp.float32)
            largest = jnp.max(scores, axis=1, keepdims=True)
            weights = jnp.exp((scores - largest) * factor)
            inverse = 1.0 / jnp.sum(weights, axis=1, keepdims=True)
            probs = (weights * inverse).astype(jnp.bfloat16)
            p_ref[h] = probs[:, fixed_len:]
            acc_ref[:, h * head_size : (h + 1) * head_size] = jnp.dot(
                probs[:, :fixed_len], vbuf[...], preferred_element_type=jnp.float32
            )

    return pl.pallas_call(
        body,
        grid_spec=pltpu.PrefetchScalarGridSpec(
            num_scalar_prefetch=1,
            grid=(per_device,),
            in_specs=[
                pl.BlockSpec((BLOCK, group * head_size), lambda i, t: (i, t[1 + turn])),
                whole(key_main),
                whole(val_main),
                whole(halo_before),
                whole(halo_after),
                whole(globs),
                pl.BlockSpec((RAND, BLOCK, head_size), lambda i, t: (side * per_device + i, 0, 0)),
            ],
            out_specs=[
                pl.BlockSpec((BLOCK, group * head_size), lambda i, t: (i, 0)),
                pl.BlockSpec((group, BLOCK, rand_len), lambda i, t: (0, i, 0)),
            ],
            scratch_shapes=[
                pltpu.VMEM((fixed_len + rand_len, head_size), jnp.bfloat16),
                pltpu.VMEM((fixed_len, head_size), jnp.bfloat16),
            ],
        ),
        out_shape=[
            jax.ShapeDtypeStruct((rows, group * head_size), jnp.float32),
            jax.ShapeDtypeStruct((group, rows, rand_len), jnp.bfloat16),
        ],
        name=name,
    )(place["table"], query, key_main, val_main, halo_before, halo_after, globs, key_rand)


def finish(partial, probs, val_rand, side, name):
    rows, width = partial.shape
    group = probs.shape[0]
    head_size = val_rand.shape[-1]
    rand_len = probs.shape[-1]
    per_device = rows // BLOCK

    def body(acc_ref, p_ref, v_ref, out_ref):
        values = v_ref[...].reshape(rand_len, head_size)
        for h in range(group):
            cols = slice(h * head_size, (h + 1) * head_size)
            more = jnp.dot(p_ref[h], values, preferred_element_type=jnp.float32)
            out_ref[:, cols] = (acc_ref[:, cols] + more).astype(out_ref.dtype)

    return pl.pallas_call(
        body,
        grid=(per_device,),
        in_specs=[
            pl.BlockSpec((BLOCK, width), lambda i: (i, 0)),
            pl.BlockSpec((group, BLOCK, rand_len), lambda i: (0, i, 0)),
            pl.BlockSpec((RAND, BLOCK, head_size), lambda i: (side * per_device + i, 0, 0)),
        ],
        out_specs=pl.BlockSpec((BLOCK, width), lambda i: (i, 0)),
        out_shape=jax.ShapeDtypeStruct((rows, width), jnp.bfloat16),
        name=name,
    )(partial, probs, val_rand)


def assemble(place_table, parts):
    rows, width = parts[0].shape

    def body(tab, *refs):
        ins, out, sems = refs[: len(parts)], refs[len(parts)], refs[len(parts) + 1]
        copies = [
            pltpu.make_async_copy(
                ins[j], out.at[:, pl.ds(pl.multiple_of((tab[3] ^ j) * width, width), width)], sems.at[j]
            )
            for j in range(len(parts))
        ]
        for copy in copies:
            copy.start()
        for copy in copies:
            copy.wait()

    return pl.pallas_call(
        body,
        grid_spec=pltpu.PrefetchScalarGridSpec(
            num_scalar_prefetch=1,
            grid=(1,),
            in_specs=[ANY] * len(parts),
            out_specs=ANY,
            scratch_shapes=[pltpu.SemaphoreType.DMA((len(parts),))],
        ),
        out_shape=jax.ShapeDtypeStruct((rows, len(parts) * width), parts[0].dtype),
        name="assemble",
    )(place_table, *parts)


def tables(rand_blocks, ctx_count, shard_blocks, per_device, capacity, me, f):
    entries = shard_blocks * RAND
    requests = rand_blocks.reshape(ctx_count, entries)
    source = requests // shard_blocks
    block = requests % shard_blocks
    block = ((block // per_device) ^ f) * per_device + block % per_device
    ids = jnp.arange(entries, dtype=jnp.int32)
    same = (source[:, :, None] == source[:, None, :]) & (ids[None, None, :] < ids[None, :, None])
    rank = jnp.sum(same.astype(jnp.int32), axis=2)
    slot = source * capacity + rank
    slots = jnp.arange(ctx_count * capacity, dtype=jnp.int32)
    hit = slot[:, None, :] == slots[None, :, None]
    picked = jnp.sum(jnp.where(hit, block[:, None, :], 0), axis=2)
    picked = picked.reshape(ctx_count, ctx_count, capacity)
    spot = ids // RAND
    spot = ((spot // per_device) ^ f) * per_device + spot % per_device
    spot = spot * RAND + ids % RAND
    mine = lax.dynamic_slice_in_dim(slot, me, 1, 0)
    target = jnp.sum(jnp.where(mine == slots[:, None], spot[None, :] + 1, 0), axis=1) - 1
    return picked, target.reshape(ctx_count, capacity)


def shards(acts, queries, kv_weight, rand_blocks):
    ctx_count = lax.axis_size("ctx")
    fsdp_count = lax.axis_size("fsdp")
    tok_rows = acts.shape[0]
    head_size = kv_weight.shape[3]
    per_device = tok_rows // BLOCK
    shard_blocks = per_device * fsdp_count
    assert fsdp_count == 4 and kv_weight.shape[1] == 1 and ctx_count & (ctx_count - 1) == 0 and GLOBAL <= per_device
    me = lax.axis_index("ctx").astype(jnp.int32)
    f = lax.axis_index("fsdp").astype(jnp.int32)
    core = f % 2
    place = {"table": jnp.stack([core, f, f ^ 2, f]), "heads": fsdp_count}
    capacity = (RAND * shard_blocks + ctx_count - 1) // ctx_count
    entries = shard_blocks * RAND
    half = entries // 2

    key_w = kv_weight[:, 0, 0, :]
    val_w = kv_weight[:, 0, 1, :]
    other_key_w = swap(key_w, "fsdp", 2)
    acts_pair = (acts, swap(acts, "fsdp", 1))
    query_pair = (queries, swap(queries, "fsdp", 1))
    other_val_w = swap(after(val_w, other_key_w), "fsdp", 2)

    def blocks(x):
        return x.reshape(-1, BLOCK, head_size)

    chip_k = blocks(project(acts_pair, key_w, "own_key"))
    chip_v = blocks(project(acts_pair, val_w, "own_value"))
    other_k = blocks(project(acts_pair, other_key_w, "other_key"))
    far_k = swap(other_k, "fsdp", 2)
    other_v = blocks(project(acts_pair, other_val_w, "other_value"))
    far_v = swap(other_v, "fsdp", 2)

    picked, target = tables(rand_blocks, ctx_count, shard_blocks, per_device, capacity, me, f)
    all_ids = jnp.arange(ctx_count, dtype=jnp.int32)
    glob_ids = f * per_device + jnp.arange(GLOBAL, dtype=jnp.int32)
    direct = ctx_count > MOST_PERMUTES

    if direct:
        mine_picks = lax.dynamic_index_in_dim(picked, me, 1, keepdims=False).reshape(-1)
        near_table = jnp.concatenate([mine_picks, glob_ids])
        goal = target.reshape(-1)

        def collect(near, tag):
            out, glob = move_blocks(near_table, near, [ctx_count * capacity, GLOBAL], False, "pick_" + tag)
            got = lax.all_to_all(out, "ctx", split_axis=0, concat_axis=0, tiled=True)
            return move_blocks(goal, [got], [half, half], True, "place_" + tag), glob
    else:
        groups = ctx_count // 2
        peers = me ^ all_ids[:groups]
        rows = picked[peers]
        near_table = lax.dynamic_index_in_dim(rows, me, 1, keepdims=False).reshape(-1)
        near_table = jnp.concatenate([near_table, glob_ids])
        far_table = lax.dynamic_index_in_dim(rows, me ^ groups, 1, keepdims=False).reshape(-1)
        goal = target[me ^ all_ids].reshape(-1)

        def collect(near, tag):
            across = [swap(x, "ctx", groups) for x in near]
            *outs, glob = move_blocks(near_table, near, [capacity] * groups + [GLOBAL], False, "pick_" + tag)
            got = [outs[0]] + [swap(outs[k], "ctx", k) for k in range(1, groups)]
            outs = move_blocks(far_table, across, [capacity] * groups, False, "pick_across_" + tag)
            got += [outs[0]] + [swap(outs[k], "ctx", k) for k in range(1, groups)]
            return move_blocks(goal, got, [half, half], True, "place_" + tag), glob

    (key_rand, key_send), key_glob = collect([chip_k, far_k], "key")
    (val_rand, val_send), val_glob = collect([chip_v, far_v], "value")
    other_key_rand = swap(key_send, "fsdp", 2)
    other_val_rand = swap(val_send, "fsdp", 2)

    globs = jnp.concatenate([key_glob, val_glob], axis=0)
    stride = ctx_count // 2
    while stride:
        pairs = [(j, j + stride) for j in range(0, ctx_count, 2 * stride)]
        came = lax.ppermute(globs, "ctx", pairs)
        globs = jnp.where(me % (2 * stride) == stride, came, globs)
        stride //= 2
    other_globs = swap(globs, "fsdp", 2)

    def end_blocks(index):
        return jnp.concatenate(
            [lax.dynamic_slice_in_dim(x, index, 1, 0) for x in (chip_k, chip_v, other_k, other_v)], axis=0
        )

    last = end_blocks((1 ^ core) * per_device + per_device - 1)
    first = end_blocks(core * per_device)
    count = ctx_count * fsdp_count
    ring = [(i, (i + 2) % count) for i in range(count)]
    halo_before = lax.ppermute(last, ("ctx", "fsdp"), ring)
    halo_after = lax.ppermute(first, ("ctx", "fsdp"), [(j, i) for i, j in ring])

    results = {}
    partials = {}
    heads = (
        (0, chip_k, chip_v, globs, key_rand, val_rand),
        (1, other_k, other_v, other_globs, other_key_rand, other_val_rand),
    )
    for turn, key_main, val_main, glob, k_rand, _ in heads:
        for side in (1, 0):
            partials[turn, side] = probabilities(
                place, query_pair[side], key_main, val_main, halo_before, halo_after, glob, k_rand, side, turn,
                f"probs_{turn}_{side}",
            )
    for turn, _, _, _, _, v_rand in heads:
        for side in (1, 0):
            results[turn, side] = finish(*partials[turn, side], v_rand, side, f"finish_{turn}_{side}")
    back = [swap(results[turn, 1], "fsdp", 1) for turn in (0, 1)]
    return assemble(place["table"], [results[0, 0], back[0], results[1, 0], back[1]])


def solution(mesh):
    placed = (P(("ctx", "fsdp"), None), P(("ctx", "fsdp"), None), P(None, "fsdp", None, None), P())
    return jax.shard_map(
        shards, mesh=mesh, in_specs=placed, out_specs=P(("ctx", "fsdp"), None), check_vma=False
    )
```

```python
import functools
import math

import jax
import jax.numpy as jnp
from jax import lax
from jax.experimental import pallas as pl
from jax.experimental.pallas import tpu as pltpu
from jax.sharding import PartitionSpec as P

BLOCK = 128
GLOBAL = 2
RAND = 3
MOST_PERMUTES = 16
STATS = 8
PARAMS = pltpu.CompilerParams(vmem_limit_bytes=24 * 2**20)


def swap(value, axis, bit):
    size = lax.axis_size(axis)
    return lax.ppermute(value, axis, [(i, i ^ bit) for i in range(size)])


def cost(flops):
    return pl.CostEstimate(flops=flops, transcendentals=0, bytes_accessed=0)


def after(value, *earlier):
    return lax.optimization_barrier((value, *earlier))[0]


def move_blocks(table, sources, out_sizes, by_target, name):
    shape = sources[0].shape[1:]
    dtype = sources[0].dtype
    source_sizes = [s.shape[0] for s in sources]
    fixed_sizes, moving_sizes = (source_sizes, out_sizes) if by_target else (out_sizes, source_sizes)

    def body(tab, *refs):
        ins, outs = refs[: len(sources)], refs[len(sources) :]
        fixed, moving = (ins, outs) if by_target else (outs, ins)
        pairs = [(ref, j) for ref, size in zip(fixed, fixed_sizes) for j in range(size)]
        for t, (ref, j) in enumerate(pairs):
            where = tab[t]
            low = 0
            for other, size in zip(moving, moving_sizes):
                @pl.when((where >= low) & (where < low + size))
                def _(other=other, low=low, ref=ref, j=j, where=where):
                    if by_target:
                        other[where - low] = ref[j]
                    else:
                        ref[j] = other[where - low]
                low += size

    return pl.pallas_call(
        body,
        grid_spec=pltpu.PrefetchScalarGridSpec(
            num_scalar_prefetch=1,
            grid=(1,),
            in_specs=[whole(x) for x in sources],
            out_specs=[pl.BlockSpec((size, *shape), lambda i, t: (0, 0, 0)) for size in out_sizes],
        ),
        out_shape=[jax.ShapeDtypeStruct((size, *shape), dtype) for size in out_sizes],
        compiler_params=PARAMS,
        name=name,
    )(table, *sources)


def split_weight(kv_weight):
    width, head_size = kv_weight.shape[0], kv_weight.shape[3]
    rows = kv_weight.reshape(2 * width, head_size)
    steps = 4
    step = width // steps

    def body(w, k_out, v_out, buf):
        buf[...] = w[...].astype(jnp.float32)
        k_out[...] = buf[pl.ds(0, step, stride=2), :].astype(k_out.dtype)
        v_out[...] = buf[pl.ds(1, step, stride=2), :].astype(v_out.dtype)

    return pl.pallas_call(
        body,
        grid=(steps,),
        in_specs=[pl.BlockSpec((2 * step, head_size), lambda i: (i, 0))],
        out_specs=[pl.BlockSpec((step, head_size), lambda i: (i, 0))] * 2,
        out_shape=[jax.ShapeDtypeStruct((width, head_size), kv_weight.dtype)] * 2,
        scratch_shapes=[pltpu.VMEM((2 * step, head_size), jnp.float32)],
        compiler_params=PARAMS,
        name="split_weight",
    )(rows)


def project(acts_pair, weights, name):
    rows, width = acts_pair[0].shape
    cols = weights[0].shape[1]
    total = cols * len(weights)
    parts = 2
    step = width // parts

    def body(mine, theirs, *refs):
        ws, outs, acc = refs[: len(weights)], refs[len(weights) : -1], refs[-1]
        turn, part = pl.program_id(0), pl.program_id(1)

        def add(ref):
            w = jnp.concatenate([w[pl.ds(pl.multiple_of(part * step, step), step), :] for w in ws], axis=1)
            term = jnp.dot(ref[...], w, preferred_element_type=jnp.float32)

            @pl.when(part == 0)
            def _():
                acc[...] = term

            @pl.when((part > 0) & (part < parts - 1))
            def _():
                acc[...] += term

            @pl.when(part == parts - 1)
            def _():
                value = acc[...] + term
                for j, out in enumerate(outs):
                    out[...] = value[:, j * cols : (j + 1) * cols].astype(out.dtype)

        pl.when(turn == 0)(lambda: add(mine))
        pl.when(turn == 1)(lambda: add(theirs))

    return pl.pallas_call(
        body,
        grid=(2, parts),
        in_specs=[
            pl.BlockSpec((rows, step), lambda i, k: (0, jnp.where(i == 0, k, parts - 1))),
            pl.BlockSpec((rows, step), lambda i, k: (0, jnp.where(i == 0, 0, k))),
        ]
        + [pl.BlockSpec((width, cols), lambda i, k: (0, 0))] * len(weights),
        out_specs=[pl.BlockSpec((rows, cols), lambda i, k: (i, 0))] * len(weights),
        out_shape=[jax.ShapeDtypeStruct((2 * rows, cols), jnp.bfloat16)] * len(weights),
        scratch_shapes=[pltpu.VMEM((rows, total), jnp.float32)],
        cost_estimate=cost(4 * rows * width * max(total, 256)),
        compiler_params=PARAMS,
        name=name,
    )(*acts_pair, *weights)


def whole(array):
    zeros = (0,) * array.ndim
    return pl.BlockSpec(array.shape, lambda i, t: zeros)


def stacked_heads(ref, i, group, head_size):
    return jnp.concatenate(
        [ref[i * BLOCK : (i + 1) * BLOCK, h * head_size : (h + 1) * head_size] for h in range(group)], axis=0
    )


def by_step(step, mine, theirs, act):
    pl.when(step == 0)(lambda: act(theirs))
    pl.when(step == 1)(lambda: act(mine))


def query_spec(rows, width, turn):
    return pl.BlockSpec((rows, width), lambda s, t: (0, t[1 + turn]))


def near_part(place, query_pair, key_main, val_main, halo_before, halo_after, globs, turn, name):
    head_size = key_main.shape[-1]
    chip_blocks = key_main.shape[0]
    per_device = chip_blocks // 2
    group = query_pair[0].shape[1] // head_size // place["heads"]
    rows = group * BLOCK
    fixed_len = (3 + GLOBAL) * BLOCK
    factor = math.log2(math.e) / math.sqrt(head_size)
    halo_at = 1 - turn
    window = 3

    def body(tab, mine, theirs, k_ref, v_ref, hb_ref, ha_ref, g_ref, acc_ref, stat_ref, line, kbuf, vbuf):
        step = pl.program_id(0)
        core = tab[0]
        start = jnp.where(step == 0, 1 ^ core, core) * per_device

        def put(at, key, value):
            line[0, at] = key
            line[1, at] = value

        for j in range(per_device + window - 1):
            at = start + j - 1

            @pl.when(at < 0)
            def _(j=j):
                put(j, hb_ref[2 * halo_at], hb_ref[2 * halo_at + 1])

            @pl.when(at >= chip_blocks)
            def _(j=j):
                put(j, ha_ref[2 * halo_at], ha_ref[2 * halo_at + 1])

            @pl.when((at >= 0) & (at < chip_blocks))
            def _(j=j, at=at):
                where = ((at // per_device) ^ core) * per_device + at % per_device
                put(j, k_ref[where], v_ref[where])

        for i in range(per_device):
            for slot in range(window):
                kbuf[i, slot * BLOCK : (slot + 1) * BLOCK, :] = line[0, i + slot]
                vbuf[i, slot * BLOCK : (slot + 1) * BLOCK, :] = line[1, i + slot]
            for g in range(GLOBAL):
                spot = slice((window + g) * BLOCK, (window + g + 1) * BLOCK)
                kbuf[i, spot, :] = g_ref[g]
                vbuf[i, spot, :] = g_ref[GLOBAL + g]

        def attend(ref):
            for i in range(per_device):
                query = stacked_heads(ref, i, group, head_size)
                scores = lax.dot_general(kbuf[i], query, (((1,), (1,)), ((), ())), preferred_element_type=jnp.float32)
                largest = jnp.max(scores, axis=0, keepdims=True)
                weights = jnp.exp2((scores - largest) * factor)
                acc_ref[i] = lax.dot_general(
                    vbuf[i], weights.astype(jnp.bfloat16), (((0,), (0,)), ((), ())), preferred_element_type=jnp.float32
                )
                stat_ref[i, 0:1, :] = largest
                stat_ref[i, 1:2, :] = jnp.sum(weights, axis=0, keepdims=True)

        by_step(step, mine, theirs, attend)

    return pl.pallas_call(
        body,
        grid_spec=pltpu.PrefetchScalarGridSpec(
            num_scalar_prefetch=1,
            grid=(2,),
            in_specs=[query_spec(per_device * BLOCK, group * head_size, turn)] * 2
            + [whole(x) for x in (key_main, val_main, halo_before, halo_after, globs)],
            out_specs=[
                pl.BlockSpec((per_device, head_size, rows), lambda s, t: (s, 0, 0)),
                pl.BlockSpec((per_device, STATS, rows), lambda s, t: (s, 0, 0)),
            ],
            scratch_shapes=[
                pltpu.VMEM((2, per_device + window - 1, BLOCK, head_size), jnp.bfloat16),
                pltpu.VMEM((per_device, fixed_len, head_size), jnp.bfloat16),
                pltpu.VMEM((per_device, fixed_len, head_size), jnp.bfloat16),
            ],
        ),
        out_shape=[
            jax.ShapeDtypeStruct((chip_blocks, head_size, rows), jnp.float32),
            jax.ShapeDtypeStruct((chip_blocks, STATS, rows), jnp.float32),
        ],
        cost_estimate=cost(chip_blocks * rows * fixed_len * head_size * 4),
        compiler_params=PARAMS,
        name=name,
    )(place["table"], *query_pair, key_main, val_main, halo_before, halo_after, globs)


def random_part(place, query_pair, stats, key_rand, turn, name):
    head_size = key_rand.shape[-1]
    chip_blocks, _, rows = stats.shape
    per_device = chip_blocks // 2
    group = rows // BLOCK
    rand_len = RAND * BLOCK
    factor = math.log2(math.e) / math.sqrt(head_size)

    def body(tab, mine, theirs, stat_ref, k_ref, p_ref, scale_ref):
        step = pl.program_id(0)

        def attend(ref):
            for i in range(per_device):
                query = stacked_heads(ref, i, group, head_size)
                keys = k_ref[i * RAND : (i + 1) * RAND].reshape(rand_len, head_size)
                scores = lax.dot_general(keys, query, (((1,), (1,)), ((), ())), preferred_element_type=jnp.float32)
                before = stat_ref[i, 0:1, :]
                largest = jnp.maximum(before, jnp.max(scores, axis=0, keepdims=True))
                weights = jnp.exp2((scores - largest) * factor)
                shrink = jnp.exp2((before - largest) * factor)
                inverse = 1.0 / (stat_ref[i, 1:2, :] * shrink + jnp.sum(weights, axis=0, keepdims=True))
                p_ref[i] = (weights * inverse).astype(jnp.bfloat16)
                scale_ref[i, 0:1, :] = shrink * inverse

        by_step(step, mine, theirs, attend)

    return pl.pallas_call(
        body,
        grid_spec=pltpu.PrefetchScalarGridSpec(
            num_scalar_prefetch=1,
            grid=(2,),
            in_specs=[query_spec(per_device * BLOCK, group * head_size, turn)] * 2
            + [
                pl.BlockSpec((per_device, STATS, rows), lambda s, t: (s, 0, 0)),
                pl.BlockSpec((per_device * RAND, BLOCK, head_size), lambda s, t: (1 - s, 0, 0)),
            ],
            out_specs=[
                pl.BlockSpec((per_device, rand_len, rows), lambda s, t: (s, 0, 0)),
                pl.BlockSpec((per_device, STATS, rows), lambda s, t: (s, 0, 0)),
            ],
        ),
        out_shape=[
            jax.ShapeDtypeStruct((chip_blocks, rand_len, rows), jnp.bfloat16),
            jax.ShapeDtypeStruct((chip_blocks, STATS, rows), jnp.float32),
        ],
        cost_estimate=cost(chip_blocks * rows * rand_len * head_size * 4),
        compiler_params=PARAMS,
        name=name,
    )(place["table"], *query_pair, stats, key_rand)


def finish(near, probs, scale, val_rand, sides, name):
    chip_blocks, head_size, rows = near.shape
    per_device = chip_blocks // 2
    group = rows // BLOCK
    rand_len = probs.shape[1]
    first = 0 if 1 in sides else 1

    def body(acc_ref, p_ref, s_ref, v_ref, *outs):
        def store(out_ref):
            for i in range(per_device):
                values = v_ref[i * RAND : (i + 1) * RAND].reshape(rand_len, head_size)
                more = lax.dot_general(values, p_ref[i], (((0,), (0,)), ((), ())), preferred_element_type=jnp.float32)
                result = acc_ref[i] * s_ref[i, 0:1, :] + more
                for h in range(group):
                    out_ref[i * BLOCK : (i + 1) * BLOCK, h * head_size : (h + 1) * head_size] = (
                        result[:, h * BLOCK : (h + 1) * BLOCK].T.astype(out_ref.dtype)
                    )

        for j, out_ref in enumerate(outs):
            pl.when(pl.program_id(0) == j)(functools.partial(store, out_ref))

    return pl.pallas_call(
        body,
        grid=(len(sides),),
        in_specs=[
            pl.BlockSpec((per_device, head_size, rows), lambda s: (s + first, 0, 0)),
            pl.BlockSpec((per_device, rand_len, rows), lambda s: (s + first, 0, 0)),
            pl.BlockSpec((per_device, STATS, rows), lambda s: (s + first, 0, 0)),
            pl.BlockSpec((per_device * RAND, BLOCK, head_size), lambda s: (1 - s - first, 0, 0)),
        ],
        out_specs=[pl.BlockSpec((per_device * BLOCK, group * head_size), lambda s: (0, 0))] * len(sides),
        out_shape=[jax.ShapeDtypeStruct((per_device * BLOCK, group * head_size), jnp.bfloat16)] * len(sides),
        cost_estimate=cost(len(sides) * per_device * rows * rand_len * head_size * 4),
        compiler_params=PARAMS,
        name=name,
    )(near, probs, scale, val_rand)


def assemble(place_table, parts):
    rows, width = parts[0].shape

    def body(tab, *refs):
        ins, out = refs[: len(parts)], refs[len(parts)]
        for j, ref in enumerate(ins):
            @pl.when(pl.program_id(0) == j)
            def _(ref=ref):
                out[...] = ref[...]

    return pl.pallas_call(
        body,
        grid_spec=pltpu.PrefetchScalarGridSpec(
            num_scalar_prefetch=1,
            grid=(len(parts),),
            in_specs=[whole(x) for x in parts],
            out_specs=pl.BlockSpec((rows, width), lambda i, t: (0, t[3] ^ i)),
        ),
        out_shape=jax.ShapeDtypeStruct((rows, len(parts) * width), parts[0].dtype),
        compiler_params=PARAMS,
        name="assemble",
    )(place_table, *parts)


def tables(rand_blocks, ctx_count, shard_blocks, per_device, capacity, me, f):
    entries = shard_blocks * RAND
    requests = rand_blocks.reshape(ctx_count, entries)
    source = requests // shard_blocks
    block = requests % shard_blocks
    block = ((block // per_device) ^ f) * per_device + block % per_device
    ids = jnp.arange(entries, dtype=jnp.int32)
    same = (source[:, :, None] == source[:, None, :]) & (ids[None, None, :] < ids[None, :, None])
    rank = jnp.sum(same.astype(jnp.int32), axis=2)
    slot = source * capacity + rank
    slots = jnp.arange(ctx_count * capacity, dtype=jnp.int32)
    hit = slot[:, None, :] == slots[None, :, None]
    picked = jnp.sum(jnp.where(hit, block[:, None, :], 0), axis=2)
    picked = picked.reshape(ctx_count, ctx_count, capacity)
    spot = ids // RAND
    spot = ((spot // per_device) ^ f) * per_device + spot % per_device
    spot = spot * RAND + ids % RAND
    mine = lax.dynamic_slice_in_dim(slot, me, 1, 0)
    target = jnp.sum(jnp.where(mine == slots[:, None], spot[None, :] + 1, 0), axis=1) - 1
    return picked, target.reshape(ctx_count, capacity)


def shards(acts, queries, kv_weight, rand_blocks):
    ctx_count = lax.axis_size("ctx")
    fsdp_count = lax.axis_size("fsdp")
    tok_rows = acts.shape[0]
    head_size = kv_weight.shape[3]
    per_device = tok_rows // BLOCK
    shard_blocks = per_device * fsdp_count
    assert fsdp_count == 4 and kv_weight.shape[1] == 1 and ctx_count & (ctx_count - 1) == 0 and GLOBAL <= per_device
    me = lax.axis_index("ctx").astype(jnp.int32)
    f = lax.axis_index("fsdp").astype(jnp.int32)
    core = f % 2
    place = {"table": jnp.stack([core, f, f ^ 2, f]), "heads": fsdp_count}
    capacity = (RAND * shard_blocks + ctx_count - 1) // ctx_count
    entries = shard_blocks * RAND
    half = entries // 2

    key_w, val_w = split_weight(kv_weight)
    other_key_w = swap(key_w, "fsdp", 2)
    acts_pair = (acts, swap(acts, "fsdp", 1))
    query_pair = (queries, swap(queries, "fsdp", 1))
    other_val_w = swap(after(val_w, other_key_w), "fsdp", 2)

    def blocks(x):
        return x.reshape(-1, BLOCK, head_size)

    chip_k, chip_v = map(blocks, project(acts_pair, [key_w, val_w], "own_heads"))
    other_k = blocks(*project(acts_pair, [after(other_key_w, chip_k)], "other_key"))
    far_k = swap(other_k, "fsdp", 2)

    picked, target = tables(rand_blocks, ctx_count, shard_blocks, per_device, capacity, me, f)
    all_ids = jnp.arange(ctx_count, dtype=jnp.int32)
    glob_ids = f * per_device + jnp.arange(GLOBAL, dtype=jnp.int32)
    direct = ctx_count > MOST_PERMUTES

    if direct:
        mine_picks = lax.dynamic_index_in_dim(picked, me, 1, keepdims=False).reshape(-1)
        near_table = jnp.concatenate([mine_picks, glob_ids])
        goal = target.reshape(-1)

        def collect(near, tag):
            out, glob = move_blocks(near_table, near, [ctx_count * capacity, GLOBAL], False, "pick_" + tag)
            got = lax.all_to_all(out, "ctx", split_axis=0, concat_axis=0, tiled=True)
            return move_blocks(goal, [got], [half, half], True, "place_" + tag), glob, glob
    else:
        groups = ctx_count // 2
        peers = me ^ all_ids[:groups]
        rows = picked[peers]
        near_table = lax.dynamic_index_in_dim(rows, me, 1, keepdims=False).reshape(-1)
        near_table = jnp.concatenate([near_table, glob_ids])
        far_table = lax.dynamic_index_in_dim(rows, me ^ groups, 1, keepdims=False).reshape(-1)
        goal = target[me ^ all_ids].reshape(-1)

        def collect(near, tag):
            across = [swap(x, "ctx", groups) for x in near]
            *outs, glob = move_blocks(near_table, near, [capacity] * groups + [GLOBAL], False, "pick_" + tag)
            got = [outs[0]] + [swap(outs[k], "ctx", k) for k in range(1, groups)]
            outs = move_blocks(far_table, across, [capacity] * groups, False, "pick_across_" + tag)
            got += [outs[0]] + [swap(outs[k], "ctx", k) for k in range(1, groups)]
            return move_blocks(goal, got, [half, half], True, "place_" + tag), glob, glob

    (key_rand, key_send), key_glob, key_token = collect([chip_k, far_k], "key")
    other_v = blocks(*project(acts_pair, [after(other_val_w, key_token)], "other_value"))
    far_v = swap(other_v, "fsdp", 2)
    (val_rand, val_send), val_glob, val_token = collect([chip_v, far_v], "value")
    other_key_rand = swap(key_send, "fsdp", 2)
    other_val_rand = swap(val_send, "fsdp", 2)

    globs = jnp.concatenate([key_glob, val_glob], axis=0)
    stride = ctx_count // 2
    while stride:
        pairs = [(j, j + stride) for j in range(0, ctx_count, 2 * stride)]
        came = lax.ppermute(globs, "ctx", pairs)
        globs = jnp.where(me % (2 * stride) == stride, came, globs)
        stride //= 2
    other_globs = swap(globs, "fsdp", 2)

    def end_blocks(index):
        return jnp.concatenate(
            [lax.dynamic_slice_in_dim(x, index, 1, 0) for x in (chip_k, chip_v, other_k, other_v)], axis=0
        )

    last = end_blocks((1 ^ core) * per_device + per_device - 1)
    first = end_blocks(core * per_device)
    count = ctx_count * fsdp_count
    ring = [(i, (i + 2) % count) for i in range(count)]
    halo_before = lax.ppermute(last, ("ctx", "fsdp"), ring)
    halo_after = lax.ppermute(first, ("ctx", "fsdp"), [(j, i) for i, j in ring])

    results = {}
    heads = (
        (0, chip_k, chip_v, globs, key_rand, val_rand),
        (1, other_k, other_v, other_globs, other_key_rand, other_val_rand),
    )
    for turn, key_main, val_main, glob, k_rand, v_rand in heads:
        near, stats = near_part(
            place, query_pair, key_main, val_main, halo_before, halo_after, glob, turn, f"near_{turn}"
        )
        probs, scale = random_part(place, query_pair, stats, k_rand, turn, f"random_{turn}")
        for sides in ((1, 0),) if turn == 0 else ((1,), (0,)):
            outs = finish(near, probs, scale, v_rand, sides, f"finish_{turn}_{sides[0]}")
            results.update({(turn, side): out for side, out in zip(sides, outs)})
    back = [swap(results[turn, 1], "fsdp", 1) for turn in (0, 1)]
    return assemble(place["table"], [results[0, 0], back[0], results[1, 0], back[1]])


def solution(mesh):
    placed = (P(("ctx", "fsdp"), None), P(("ctx", "fsdp"), None), P(None, "fsdp", None, None), P())
    return jax.shard_map(
        shards, mesh=mesh, in_specs=placed, out_specs=P(("ctx", "fsdp"), None), check_vma=False
    )
```
